512 devices in a mesh: row: 16 (over x_hi, y), col: 32 (over z, x_lo, core).
Axes of the slice: x: 4 (x_hi: 2, x_lo: 2; x = x_hi * 2 + x_lo), y: 8, z: 8, core: 2. Of those that a mesh axis runs over, the one named last changes fastest.
Arguments:
- base_input: bfloat16 [1024, 16384], P('col', 'row'), may hold values from -6 to 6
- layer_input: bfloat16 [1024, 16384], P('row', 'col'), may hold values from -6 to 6
- out_grad: bfloat16 [1024, 16384], P('col', 'row'), may hold values from -6 to 6
- cross_weight: bfloat16 [16384, 16384], P('row', 'col'), may hold values from -0.046875 to 0.046875
- cross_bias: bfloat16 [16384], P('row'), may hold values from -5 to 5
Outputs:
- weight_grad: float32 [16384, 16384], P('row', 'col')
- bias_grad: float32 [16384], P('row')
- base_grad: bfloat16 [1024, 16384], P('col', 'row')
- branch_grad: bfloat16 [1024, 16384], P('row', 'col')
The draws below stay inside these ranges and needn't reach their ends.
All inputs are finite; a program needn't handle non-finite values.
Results may differ from the reference program's by a relative error of at most 0.019.
Values may be sent and summed in bfloat16 or wider, within the bound.
A program may use at most 64 MiB of HBM per device.

```python
import jax
import jax.numpy as jnp
from jax import lax

D = 16384
EXAMPLES = 1024
N_ROW = 16
N_COL = 32


def steps_of(key, dims, shards, smallest, largest):
    level, own = 1.0, jax.random.fold_in(key, 6)
    for axis_at, shards_of in shards:
        steps = jnp.exp(jax.random.uniform(jax.random.fold_in(own, axis_at), (shards_of,), jnp.float32, smallest / len(shards), largest / len(shards)))
        level = level * jnp.repeat(steps, dims[axis_at] // shards_of).reshape([-1 if axis == axis_at else 1 for axis in range(len(dims))])
    return level


def centred(own_key, shape, deviation, reach, shards=(), held_as=jnp.bfloat16):
    entries = jax.random.normal(own_key, shape, jnp.float32) * deviation
    if len(shards) > 0:
        entries = steps_of(own_key, shape, shards, -0.22, 0.18) * entries
    return jnp.clip(entries, min=-reach, max=reach).astype(held_as)


def setup_inputs(seed: int = 0) -> dict:
    arg_keys = jax.random.split(jax.random.key(seed), 6)
    base_input = centred(arg_keys[0], (EXAMPLES, D), 1.0, 6.0, ((0, 32), (1, 16)))
    layer_input = centred(arg_keys[1], (EXAMPLES, D), 1.0, 6.0, ((0, 16), (1, 32)))
    out_grad = centred(arg_keys[2], (EXAMPLES, D), 1.0, 6.0, ((0, 32), (1, 16)))
    cross_weight = centred(arg_keys[3], (D, D), D ** -0.5, 0.046875, ((0, 16), (1, 32)))
    cross_bias = centred(arg_keys[4], (D,), 1.0, 5.0, ((0, 16),))
    return {"base_input": base_input, "layer_input": layer_input, "out_grad": out_grad, "cross_weight": cross_weight, "cross_bias": cross_bias}


def reference(base_input, layer_input, out_grad, cross_weight, cross_bias):
    hidden_grad = (out_grad.astype(jnp.float32) * base_input.astype(jnp.float32)).astype(jnp.bfloat16)
    weight_grad = jnp.dot(hidden_grad.T, layer_input, preferred_element_type=jnp.float32)
    bias_grad = jnp.sum(hidden_grad.astype(jnp.float32), axis=0)
    in_block = D // N_COL
    out_block = D // N_ROW

    def pre_step(total, index):
        start = (index * in_block).astype(jnp.int32)
        rows = lax.dynamic_slice_in_dim(layer_input, start, in_block, 1)
        cols = lax.dynamic_slice_in_dim(cross_weight, start, in_block, 1)
        part = jnp.dot(rows, cols.T, preferred_element_type=jnp.float32).astype(jnp.bfloat16)
        return total + part.astype(jnp.float32), None

    zeros = jnp.zeros((EXAMPLES, D), jnp.float32)
    preact, _ = lax.scan(pre_step, zeros, jnp.arange(N_COL, dtype=jnp.int32))
    preact = preact + cross_bias.astype(jnp.float32)[None, :]
    base_grad = (out_grad.astype(jnp.float32) * preact).astype(jnp.bfloat16)

    def back_step(total, index):
        start = (index * out_block).astype(jnp.int32)
        rows = lax.dynamic_slice_in_dim(hidden_grad, start, out_block, 1)
        block = lax.dynamic_slice_in_dim(cross_weight, start, out_block, 0)
        part = jnp.dot(rows, block, preferred_element_type=jnp.float32).astype(jnp.bfloat16)
        return total + part.astype(jnp.float32), None

    branch, _ = lax.scan(back_step, zeros, jnp.arange(N_ROW, dtype=jnp.int32))
    branch_grad = branch.astype(jnp.bfloat16)
    return (weight_grad, bias_grad, base_grad, branch_grad)
```

```python
import jax
import jax.numpy as jnp
from jax import lax
from jax.experimental import pallas as pl
from jax.experimental.pallas import tpu as pltpu
from jax.sharding import PartitionSpec as P

F32, BF16 = jnp.float32, jnp.bfloat16
NZ = NY = 8
HOPS = 4
PIECES = 4


def cross_backward(
    base_hbm, inp_hbm, grad_hbm, w_hbm, bias_ref,
    wg_hbm, bg_ref, baseg_ref, branch_ref,
    base, grad, w, wt, hid, inp, pre, pre_in, back, wg,
    c_first, c_slot, c_xout, c_xin, r_first, r_slot, r_xout, r_xin,
    in_sem, out_sem,
    cg_s, cg_r, rg_s, rg_r, x_s, x_r, pg_s, pg_r,
    cs_s, cs_r, rs_s, rs_r, ps_s, ps_r, fx_s, fx_r,
):
    row, col = lax.axis_index("row"), lax.axis_index("col")
    xh, y = row // NY, lax.rem(row, NY)
    z, xl, core = col // 4, lax.rem(col // 2, 2), lax.rem(col, 2)

    def col_of(zz, xx, kk):
        return zz * 4 + xx * 2 + kk

    def at_z(d):
        return lax.rem(z + (d + NZ), NZ)

    def at_y(d):
        return lax.rem(y + (d + NY), NY)

    side = (1, -1)
    z_id = [(row, col_of(at_z(d), xl, core)) for d in side]
    y_id = [(xh * NY + at_y(d), col) for d in side]
    xl_id = (row, col_of(z, 1 - xl, core))
    core_id = (row, col_of(z, xl, 1 - core))
    xh_id = ((1 - xh) * NY + y, col)
    xls = (xl, 1 - xl)
    xhs = (xh, 1 - xh)
    sent = []

    def send(src, dst, s_sem, r_sem, to):
        copy = pltpu.make_async_remote_copy(
            src_ref=src, dst_ref=dst, send_sem=s_sem, recv_sem=r_sem,
            device_id=to, device_id_type=pl.DeviceIdType.MESH,
        )
        copy.start()
        sent.append(copy)
        return copy

    loads = [
        pltpu.make_async_copy(grad_hbm, grad, in_sem.at[0]),
        pltpu.make_async_copy(base_hbm, base, in_sem.at[1]),
        pltpu.make_async_copy(inp_hbm, inp.at[row], in_sem.at[2]),
        pltpu.make_async_copy(w_hbm, w, in_sem.at[3]),
    ]
    for load in loads:
        load.start()
    barrier = pltpu.get_barrier_semaphore()
    for to in (*z_id, *y_id, xl_id, core_id, xh_id):
        pl.semaphore_signal(barrier, inc=1, device_id=to, device_id_type=pl.DeviceIdType.MESH)
    loads[0].wait()
    loads[1].wait()
    hid[col] = (grad[...].astype(F32) * base[...].astype(F32)).astype(BF16)
    loads[2].wait()
    pl.semaphore_wait(barrier, 7)

    cg, rg, pg = {}, {}, {}

    def col_block(d, j, s):
        return col_of(at_z(-d * s), xls[j], core)

    def row_block(d, j, s):
        return xhs[j] * NY + at_y(-d * s)

    def half(ref, rows, i, last):
        return ref.at[pl.ds(i * (rows // 2), rows // 2)] if last else ref

    def gather_col(i, j, s):
        blk = half(hid.at[col_block(side[i], j, s - 1)], 32, i, s == HOPS)
        cg[i, j, s] = send(blk, blk, cg_s.at[i, j, s - 1], cg_r.at[i, j, s - 1], z_id[i])

    def gather_row(i, j, s):
        blk = half(inp.at[row_block(side[i], j, s - 1)], 64, i, s == HOPS)
        rg[i, j, s] = send(blk, blk, rg_s.at[i, j, s - 1], rg_r.at[i, j, s - 1], y_id[i])

    def share(zz, j, n):
        blk = hid.at[col_of(zz, xls[j], core)]
        pg[n, j] = send(blk, blk, pg_s.at[n, j], pg_r.at[n, j], core_id)

    x_col = send(hid.at[col], hid.at[col], x_s.at[0], x_r.at[0], xl_id)
    x_row = send(inp.at[row], inp.at[row], x_s.at[1], x_r.at[1], xh_id)
    for i in range(2):
        gather_col(i, 0, 1)
        gather_row(i, 0, 1)
    share(z, 0, 0)
    loads[3].wait()
    wt[...] = w[...].T
    x_col.wait_recv()
    for i in range(2):
        gather_col(i, 1, 1)
    share(z, 1, 0)
    x_row.wait_recv()
    for i in range(2):
        gather_row(i, 1, 1)

    ps = {}

    def pre_rows(ys):
        blocks = [xx * NY + yy for yy in ys for xx in (0, 1)]
        lhs = jnp.concatenate([inp[b] for b in blocks], axis=0)
        part = jnp.dot(lhs, wt[...], preferred_element_type=F32).astype(BF16)
        for n, b in enumerate(blocks):
            pre[b] = part[n * 64 : (n + 1) * 64]

    def merge_out(ys, base_n):
        n = base_n
        for yy in ys:
            for xx in (0, 1):
                b = xx * NY + yy
                ps[n] = send(
                    pre.at[b, pl.ds((1 - core) * 32, 32)], pre_in.at[b], ps_s.at[n], ps_r.at[n], core_id
                )
                n += 1

    def back_rows(zs):
        lhs = jnp.concatenate([hid[pl.ds(zz * 4, 4)].reshape(128, 1024) for zz in zs], axis=0)
        part = jnp.dot(lhs, w[...], preferred_element_type=F32).astype(BF16)
        for n, zz in enumerate(zs):
            back[pl.ds(zz * 2, 2)] = part[n * 128 : (n + 1) * 128].reshape(2, 64, 512)

    pre_rows([y])
    merge_out([y], 0)
    for s in range(1, HOPS + 1):
        for j in range(2):
            for i in range(2):
                cg[i, j, s].wait_recv()
                if s < HOPS:
                    gather_col(i, j, s + 1)
                    share(at_z(-side[i] * s), j, 2 * s - 1 + i)
            if s == HOPS:
                share(at_z(HOPS), j, 7)
            for i in range(2):
                rg[i, j, s].wait_recv()
                if s < HOPS:
                    gather_row(i, j, s + 1)
        if s < HOPS:
            pre_rows([at_y(-s), at_y(s)])
            merge_out([at_y(-s), at_y(s)], 2 + 4 * (s - 1))
            if s == 1:
                for j in range(2):
                    pg[0, j].wait_recv()
                back_rows([z])
            else:
                for j in range(2):
                    pg[2 * s - 3, j].wait_recv()
                    pg[2 * s - 2, j].wait_recv()
                back_rows([at_z(-(s - 1)), at_z(s - 1)])
    pre_rows([at_y(HOPS)])
    merge_out([at_y(HOPS)], 14)
    for j in range(2):
        pg[5, j].wait_recv()
        pg[6, j].wait_recv()
        pg[7, j].wait_recv()
    back_rows([at_z(-3), at_z(3), at_z(HOPS)])
    for n in range(16):
        ps[n].wait_recv()

    cs, rs = {}, {}
    mine = pl.ds(pl.multiple_of(core * 32, 32), 32)

    def pre_sum(zz, j, rows=None):
        b = zz * 2 + xls[j]
        if rows is None:
            return pre[b, mine].astype(F32) + pre_in[b].astype(F32)
        start, size = rows
        return pre[b, pl.ds(pl.multiple_of(core * 32 + start, 16), size)].astype(F32) + pre_in[
            b, pl.ds(start, size)
        ].astype(F32)

    def scatter_col(i, j, s):
        zz = at_z(side[i] * (HOPS + 1 - s))
        if s == 1:
            src, dst = c_first.at[i, j], c_slot.at[i, j, 0, pl.ds(i * 16, 16)]
            c_first[i, j] = pre_sum(zz, j, (i * 16, 16)).astype(BF16)
        else:
            slot = c_slot.at[i, j, s - 2]
            src, dst = slot, c_slot.at[i, j, s - 1]
            if s == 2:
                o = 1 - i
                own = pre_sum(zz, j, (i * 16, 16)) + slot[pl.ds(i * 16, 16)].astype(F32)
                slot[pl.ds(i * 16, 16)] = own.astype(BF16)
                slot[pl.ds(o * 16, 16)] = pre_sum(zz, j, (o * 16, 16)).astype(BF16)
            else:
                slot[...] = (pre_sum(zz, j) + slot[...].astype(F32)).astype(BF16)
        cs[i, j, s] = send(src, dst, cs_s.at[i, j, s - 1], cs_r.at[i, j, s - 1], z_id[i])

    def scatter_row(i, j, s):
        b = xhs[j] * NY + at_y(side[i] * (HOPS + 1 - s))
        if s == 1:
            src, dst = r_first.at[i, j], r_slot.at[i, j, 0, pl.ds(i * 32, 32)]
            r_first[i, j] = back[b, pl.ds(i * 32, 32)]
        else:
            slot = r_slot.at[i, j, s - 2]
            src, dst = slot, r_slot.at[i, j, s - 1]
            if s == 2:
                mid, oth = pl.ds(i * 32, 32), pl.ds((1 - i) * 32, 32)
                slot[mid] = (back[b, mid].astype(F32) + slot[mid].astype(F32)).astype(BF16)
                slot[oth] = back[b, oth]
            else:
                slot[...] = (back[b].astype(F32) + slot[...].astype(F32)).astype(BF16)
        rs[i, j, s] = send(src, dst, rs_s.at[i, j, s - 1], rs_r.at[i, j, s - 1], y_id[i])

    for j in (1, 0):
        for i in range(2):
            scatter_col(i, j, 1)
        for i in range(2):
            scatter_row(i, j, 1)

    outs = []
    width = 1024 // PIECES

    def weight_piece(n):
        cols = slice(n * width, (n + 1) * width)
        lhs = hid[:, :, cols].reshape(1024, width)
        wg[cols] = lax.dot_general(
            lhs, inp[...].reshape(1024, 512), (((0,), (0,)), ((), ())), preferred_element_type=F32
        )
        copy = pltpu.make_async_copy(wg.at[cols], wg_hbm.at[cols], out_sem.at[n])
        copy.start()
        outs.append(copy)

    weight_piece(0)
    for s in range(1, HOPS):
        for j in (1, 0):
            for i in range(2):
                cs[i, j, s].wait_recv()
                scatter_col(i, j, s + 1)
            for i in range(2):
                rs[i, j, s].wait_recv()
                scatter_row(i, j, s + 1)
        weight_piece(s)
    bg_ref[...] = jnp.sum(
        jnp.sum(hid[...].reshape(128, 8, 1024).astype(F32), axis=0), axis=0, keepdims=True
    )

    def col_total(j):
        total = pre_sum(z, j)
        for i in range(2):
            cs[i, j, HOPS].wait_recv()
            total = total + c_slot[i, j, HOPS - 1].astype(F32)
        return total

    def row_total(j):
        total = back[xhs[j] * NY + y].astype(F32)
        for i in range(2):
            rs[i, j, HOPS].wait_recv()
            total = total + r_slot[i, j, HOPS - 1].astype(F32)
        return total

    c_xout[...] = col_total(1).astype(BF16)
    fx_col = send(c_xout, c_xin, fx_s.at[0], fx_r.at[0], xl_id)
    r_xout[...] = row_total(1).astype(BF16)
    fx_row = send(r_xout, r_xin, fx_s.at[1], fx_r.at[1], xh_id)
    preact = col_total(0)
    branch = row_total(0)
    fx_col.wait_recv()
    preact = preact + c_xin[...].astype(F32) + bias_ref[...].astype(F32)
    baseg_ref[...] = (grad[...].astype(F32) * preact).astype(BF16)
    fx_row.wait_recv()
    branch_ref[...] = (branch + r_xin[...].astype(F32)).astype(BF16)
    for copy in outs:
        copy.wait()
    for copy in sent:
        copy.wait_send()


def on_device(base_input, layer_input, out_grad, cross_weight, cross_bias):
    dma = pltpu.SemaphoreType.DMA
    hbm, vmem = pl.BlockSpec(memory_space=pl.ANY), pl.BlockSpec(memory_space=pltpu.VMEM)
    weight_grad, bias_grad, base_grad, branch_grad = pl.pallas_call(
        cross_backward,
        out_shape=(
            jax.ShapeDtypeStruct((1024, 512), F32),
            jax.ShapeDtypeStruct((1, 1024), F32),
            jax.ShapeDtypeStruct((32, 1024), BF16),
            jax.ShapeDtypeStruct((64, 512), BF16),
        ),
        in_specs=[hbm, hbm, hbm, hbm, vmem],
        out_specs=(hbm, vmem, vmem, vmem),
        scratch_shapes=[
            pltpu.VMEM((32, 1024), BF16),
            pltpu.VMEM((32, 1024), BF16),
            pltpu.VMEM((1024, 512), BF16),
            pltpu.VMEM((512, 1024), BF16),
            pltpu.VMEM((32, 32, 1024), BF16),
            pltpu.VMEM((16, 64, 512), BF16),
            pltpu.VMEM((16, 64, 1024), BF16),
            pltpu.VMEM((16, 32, 1024), BF16),
            pltpu.VMEM((16, 64, 512), BF16),
            pltpu.VMEM((1024, 512), F32),
            pltpu.VMEM((2, 2, 16, 1024), BF16),
            pltpu.VMEM((2, 2, 4, 32, 1024), BF16),
            pltpu.VMEM((32, 1024), BF16),
            pltpu.VMEM((32, 1024), BF16),
            pltpu.VMEM((2, 2, 32, 512), BF16),
            pltpu.VMEM((2, 2, 4, 64, 512), BF16),
            pltpu.VMEM((64, 512), BF16),
            pltpu.VMEM((64, 512), BF16),
            dma((4,)), dma((PIECES,)),
            dma((2, 2, 4)), dma((2, 2, 4)), dma((2, 2, 4)), dma((2, 2, 4)), dma((2,)), dma((2,)), dma((8, 2)), dma((8, 2)),
            dma((2, 2, 4)), dma((2, 2, 4)), dma((2, 2, 4)), dma((2, 2, 4)), dma((16,)), dma((16,)), dma((2,)), dma((2,)),
        ],
        compiler_params=pltpu.CompilerParams(
            collective_id=0, has_side_effects=True, vmem_limit_bytes=40 << 20
        ),
    )(base_input, layer_input, out_grad, cross_weight, cross_bias.reshape(1, 1024))
    return weight_grad, bias_grad.reshape(1024), base_grad, branch_grad


def solution(mesh):
    in_specs = (P("col", "row"), P("row", "col"), P("col", "row"), P("row", "col"), P("row"))
    out_specs = (P("row", "col"), P("row"), P("col", "row"), P("row", "col"))
    return jax.shard_map(
        on_device, mesh=mesh, in_specs=in_specs, out_specs=out_specs, check_vma=False
    )
```

```python
import jax
import jax.numpy as jnp
from jax import lax
from jax.experimental import pallas as pl
from jax.experimental.pallas import tpu as pltpu
from jax.sharding import PartitionSpec as P

F32, BF16 = jnp.float32, jnp.bfloat16
NZ = NY = 8
HOPS = 4
PIECES = 8


def cross_backward(
    base_hbm, inp_hbm, grad_hbm, w_hbm, bias_hbm,
    wg_ref, bg_ref, baseg_ref, branch_ref,
    base, grad, w, wt, hid, inp, pre, pre_in, back, bias,
    c_slot, c_xout, c_xin, r_slot, r_xout, r_xin,
    in_sem,
    cg_s, cg_r, rg_s, rg_r, x_s, x_r, pg_s, pg_r,
    cs_s, cs_r, rs_s, rs_r, ps_s, ps_r, fx_s, fx_r,
):
    row, col = lax.axis_index("row"), lax.axis_index("col")
    xh, y = row // NY, lax.rem(row, NY)
    z, xl, core = col // 4, lax.rem(col // 2, 2), lax.rem(col, 2)

    def col_of(zz, xx, kk):
        return zz * 4 + xx * 2 + kk

    def at_z(d):
        return lax.rem(z + (d + NZ), NZ)

    def at_y(d):
        return lax.rem(y + (d + NY), NY)

    side = (1, -1)
    z_id = [(row, col_of(at_z(d), xl, core)) for d in side]
    y_id = [(xh * NY + at_y(d), col) for d in side]
    xl_id = (row, col_of(z, 1 - xl, core))
    core_id = (row, col_of(z, xl, 1 - core))
    xh_id = ((1 - xh) * NY + y, col)
    xls = (xl, 1 - xl)
    xhs = (xh, 1 - xh)
    sent = []

    def send(src, dst, s_sem, r_sem, to):
        copy = pltpu.make_async_remote_copy(
            src_ref=src, dst_ref=dst, send_sem=s_sem, recv_sem=r_sem,
            device_id=to, device_id_type=pl.DeviceIdType.MESH,
        )
        copy.start()
        sent.append(copy)
        return copy

    loads = [
        pltpu.make_async_copy(grad_hbm, grad, in_sem.at[0]),
        pltpu.make_async_copy(base_hbm, base, in_sem.at[1]),
        pltpu.make_async_copy(inp_hbm, inp.at[row], in_sem.at[2]),
        pltpu.make_async_copy(w_hbm, w, in_sem.at[3]),
        pltpu.make_async_copy(bias_hbm, bias, in_sem.at[4]),
    ]
    for load in loads:
        load.start()
    barrier = pltpu.get_barrier_semaphore()
    for to in (*z_id, *y_id, xl_id, core_id, xh_id):
        pl.semaphore_signal(barrier, inc=1, device_id=to, device_id_type=pl.DeviceIdType.MESH)
    loads[0].wait()
    loads[1].wait()
    hid[col] = (grad[...].astype(F32) * base[...].astype(F32)).astype(BF16)
    loads[2].wait()
    pl.semaphore_wait(barrier, 7)

    cg, rg, pg, ps = {}, {}, {}, {}
    order = [(j, q) for j in range(2) for q in range(2)]

    def col_part(ref, q):
        return ref.at[pl.ds(q * 16, 16)]

    def row_part(ref, q):
        return ref.at[pl.ds(q * 32, 32)]

    def dirs(q, last):
        return (q,) if last else (0, 1)

    def gather_col(i, j, q, s):
        blk = col_part(hid.at[col_of(at_z(-side[i] * (s - 1)), xls[j], core)], q)
        cg[i, j, q, s] = send(blk, blk, cg_s.at[i, j, q, s - 1], cg_r.at[i, j, q, s - 1], z_id[i])

    def gather_row(i, j, q, s):
        blk = row_part(inp.at[xhs[j] * NY + at_y(-side[i] * (s - 1))], q)
        rg[i, j, q, s] = send(blk, blk, rg_s.at[i, j, q, s - 1], rg_r.at[i, j, q, s - 1], y_id[i])

    def share(zz, j, n):
        blk = hid.at[col_of(zz, xls[j], core)]
        pg[n, j] = send(blk, blk, pg_s.at[n, j], pg_r.at[n, j], core_id)

    def arrive(j, q, s):
        for i in dirs(q, s == HOPS):
            cg[i, j, q, s].wait_recv()
            if s < HOPS and i in dirs(q, s + 1 == HOPS):
                gather_col(i, j, q, s + 1)
        if q == 1:
            if s == HOPS:
                share(at_z(HOPS), j, 7)
            else:
                for i in range(2):
                    share(at_z(-side[i] * s), j, 2 * s - 1 + i)
        for i in dirs(q, s == HOPS):
            rg[i, j, q, s].wait_recv()
            if s < HOPS and i in dirs(q, s + 1 == HOPS):
                gather_row(i, j, q, s + 1)

    def pre_rows(ys, base_n):
        blocks = [xx * NY + yy for yy in ys for xx in (0, 1)]
        lhs = jnp.concatenate([inp[b] for b in blocks], axis=0)
        part = jnp.dot(lhs, wt[...], preferred_element_type=F32).astype(BF16)
        for n, b in enumerate(blocks):
            pre[b] = part[n * 64 : (n + 1) * 64]
        for n, b in enumerate(blocks, base_n):
            ps[n] = send(
                pre.at[b, pl.ds((1 - core) * 32, 32)], pre_in.at[b], ps_s.at[n], ps_r.at[n], core_id
            )

    def back_rows(zs, shares):
        for n in shares:
            for j in range(2):
                pg[n, j].wait_recv()
        lhs = jnp.concatenate([hid[pl.ds(zz * 4, 4)].reshape(128, 1024) for zz in zs], axis=0)
        part = jnp.dot(lhs, w[...], preferred_element_type=F32).astype(BF16)
        for n, zz in enumerate(zs):
            back[pl.ds(zz * 2, 2)] = part[n * 128 : (n + 1) * 128].reshape(2, 64, 512)

    for q in range(2):
        for i in range(2):
            gather_col(i, 0, q, 1)
            gather_row(i, 0, q, 1)
    x_col, x_row = {}, {}
    for q in range(2):
        blk = col_part(hid.at[col], q)
        x_col[q] = send(blk, blk, x_s.at[0, q], x_r.at[0, q], xl_id)
        blk = row_part(inp.at[row], q)
        x_row[q] = send(blk, blk, x_s.at[1, q], x_r.at[1, q], xh_id)
    share(z, 0, 0)
    loads[3].wait()
    loads[4].wait()
    wt[...] = w[...].T
    for c in range(HOPS + 1):
        if c < HOPS:
            for q in range(2):
                arrive(0, q, c + 1)
        if c == 1:
            pre_rows([y], 0)
        elif c > 1:
            pre_rows([at_y(1 - c), at_y(c - 1)], 4 * c - 6)
        for q in range(2):
            if c == 0:
                x_col[q].wait_recv()
                for i in range(2):
                    gather_col(i, 1, q, 1)
                if q == 1:
                    share(z, 1, 0)
                x_row[q].wait_recv()
                for i in range(2):
                    gather_row(i, 1, q, 1)
            else:
                arrive(1, q, c)
        if c == 1:
            back_rows([z], [0])
        elif c > 1 and c < HOPS:
            back_rows([at_z(1 - c), at_z(c - 1)], [2 * c - 3, 2 * c - 2])
    pre_rows([at_y(HOPS)], 14)
    back_rows([at_z(-3), at_z(3), at_z(HOPS)], [5, 6, 7])

    cs, rs = {}, {}

    def pre_sum(zz, j, q):
        b = zz * 2 + xls[j]
        own = pre[b, pl.ds(pl.multiple_of(core * 32 + q * 16, 16), 16)]
        return own.astype(F32) + pre_in[b, pl.ds(q * 16, 16)].astype(F32)

    def scatter_col(i, j, q, s):
        slot = c_slot.at[i, j, q, s - 1]
        total = pre_sum(at_z(side[i] * (HOPS + 1 - s)), j, q)
        if s > 2 or (s == 2 and q == i):
            cs[i, j, q, s - 1].wait_recv()
            total = total + slot[...].astype(F32)
        slot[...] = total.astype(BF16)
        cs[i, j, q, s] = send(
            slot, c_slot.at[i, j, q, s], cs_s.at[i, j, q, s - 1], cs_r.at[i, j, q, s - 1], z_id[i]
        )

    def scatter_row(i, j, q, s):
        slot = r_slot.at[i, j, q, s - 1]
        own = back[xhs[j] * NY + at_y(side[i] * (HOPS + 1 - s)), pl.ds(q * 32, 32)]
        if s > 2 or (s == 2 and q == i):
            rs[i, j, q, s - 1].wait_recv()
            own = (own.astype(F32) + slot[...].astype(F32)).astype(BF16)
        slot[...] = own
        rs[i, j, q, s] = send(
            slot, r_slot.at[i, j, q, s], rs_s.at[i, j, q, s - 1], rs_r.at[i, j, q, s - 1], y_id[i]
        )

    width = 1024 // PIECES

    def weight_piece(n):
        cols = slice(n * width, (n + 1) * width)
        lhs = hid[:, :, cols].reshape(1024, width)
        wg_ref[cols] = lax.dot_general(
            lhs, inp[...].reshape(1024, 512), (((0,), (0,)), ((), ())), preferred_element_type=F32
        )

    for j in (1, 0):
        for i in range(2):
            scatter_row(i, j, i, 1)
    for n in range(16):
        ps[n].wait_recv()
    for j in (1, 0):
        for i in range(2):
            scatter_col(i, j, i, 1)
    for j in (1, 0):
        for i in range(2):
            scatter_col(i, j, 1 - i, 2)
            scatter_row(i, j, 1 - i, 2)
    weight_piece(0)
    weight_piece(1)
    for s in range(2, HOPS + 1):
        for j in (1, 0):
            for q in range(2):
                for i in range(2):
                    if s > 2 or q == i:
                        scatter_col(i, j, q, s)
                for i in range(2):
                    if s > 2 or q == i:
                        scatter_row(i, j, q, s)
            weight_piece(2 * s - 2 + (1 - j))

    def col_total(j, q):
        total = pre_sum(z, j, q)
        for i in range(2):
            cs[i, j, q, HOPS].wait_recv()
            total = total + c_slot[i, j, q, HOPS].astype(F32)
        return total

    def row_total(j, q):
        total = back[xhs[j] * NY + y, pl.ds(q * 32, 32)].astype(F32)
        for i in range(2):
            rs[i, j, q, HOPS].wait_recv()
            total = total + r_slot[i, j, q, HOPS].astype(F32)
        return total

    fx_col, fx_row = {}, {}
    for q in range(2):
        col_part(c_xout, q)[...] = col_total(1, q).astype(BF16)
        fx_col[q] = send(col_part(c_xout, q), col_part(c_xin, q), fx_s.at[0, q], fx_r.at[0, q], xl_id)
        row_part(r_xout, q)[...] = row_total(1, q).astype(BF16)
        fx_row[q] = send(row_part(r_xout, q), row_part(r_xin, q), fx_s.at[1, q], fx_r.at[1, q], xh_id)
    bg_ref[...] = jnp.sum(jnp.sum(hid[...].reshape(128, 8, 1024).astype(F32), axis=0), axis=0)
    preact = [col_total(0, q) for q in range(2)]
    branch = [row_total(0, q) for q in range(2)]
    for q in range(2):
        part = pl.ds(q * 16, 16)
        fx_col[q].wait_recv()
        total = preact[q] + c_xin[part].astype(F32) + bias[...].astype(F32)[None]
        baseg_ref[part] = (grad[part].astype(F32) * total).astype(BF16)
    for q in range(2):
        part = pl.ds(q * 32, 32)
        fx_row[q].wait_recv()
        branch_ref[part] = (branch[q] + r_xin[part].astype(F32)).astype(BF16)
    for copy in sent:
        copy.wait_send()


def write_out(*refs):
    sems = refs[8]
    copies = [pltpu.make_async_copy(refs[n], refs[4 + n], sems.at[n]) for n in range(4)]
    for copy in copies:
        copy.start()
    for copy in copies:
        copy.wait()


OUT_SHAPES = (
    jax.ShapeDtypeStruct((1024, 512), F32),
    jax.ShapeDtypeStruct((1024,), F32),
    jax.ShapeDtypeStruct((32, 1024), BF16),
    jax.ShapeDtypeStruct((64, 512), BF16),
)


def on_device(*args):
    dma = pltpu.SemaphoreType.DMA
    hbm, vmem = pl.BlockSpec(memory_space=pltpu.HBM), pl.BlockSpec(memory_space=pltpu.VMEM)
    any_space = pl.BlockSpec(memory_space=pl.ANY)
    results = pl.pallas_call(
        cross_backward,
        out_shape=OUT_SHAPES,
        in_specs=[hbm] * 5,
        out_specs=(vmem,) * 4,
        scratch_shapes=[
            pltpu.VMEM((32, 1024), BF16),
            pltpu.VMEM((32, 1024), BF16),
            pltpu.VMEM((1024, 512), BF16),
            pltpu.VMEM((512, 1024), BF16),
            pltpu.VMEM((32, 32, 1024), BF16),
            pltpu.VMEM((16, 64, 512), BF16),
            pltpu.VMEM((16, 64, 1024), BF16),
            pltpu.VMEM((16, 32, 1024), BF16),
            pltpu.VMEM((16, 64, 512), BF16),
            pltpu.VMEM((1024,), BF16),
            pltpu.VMEM((2, 2, 2, 5, 16, 1024), BF16),
            pltpu.VMEM((32, 1024), BF16),
            pltpu.VMEM((32, 1024), BF16),
            pltpu.VMEM((2, 2, 2, 5, 32, 512), BF16),
            pltpu.VMEM((64, 512), BF16),
            pltpu.VMEM((64, 512), BF16),
            dma((5,)),
            dma((2, 2, 2, 4)), dma((2, 2, 2, 4)), dma((2, 2, 2, 4)), dma((2, 2, 2, 4)), dma((2, 2)), dma((2, 2)), dma((8, 2)), dma((8, 2)),
            dma((2, 2, 2, 4)), dma((2, 2, 2, 4)), dma((2, 2, 2, 4)), dma((2, 2, 2, 4)), dma((16,)), dma((16,)), dma((2, 2)), dma((2, 2)),
        ],
        compiler_params=pltpu.CompilerParams(
            collective_id=0, has_side_effects=True, vmem_limit_bytes=40 << 20
        ),
    )(*(pltpu.with_memory_space_constraint(a, pltpu.HBM) for a in args))
    return pl.pallas_call(
        write_out,
        out_shape=OUT_SHAPES,
        in_specs=[any_space] * 4,
        out_specs=(any_space,) * 4,
        scratch_shapes=[dma((4,))],
    )(*(pltpu.with_memory_space_constraint(a, pltpu.VMEM) for a in results))


def solution(mesh):
    in_specs = (P("col", "row"), P("row", "col"), P("col", "row"), P("row", "col"), P("row"))
    out_specs = (P("row", "col"), P("row"), P("col", "row"), P("row", "col"))
    return jax.shard_map(
        on_device, mesh=mesh, in_specs=in_specs, out_specs=out_specs, check_vma=False
    )
```
